32 devices in a mesh: tile: 8 (over z, y), band: 4 (over x, core).
Axes of the slice: x: 2, y: 2, z: 4, core: 2. Of those that a mesh axis runs over, the one named last changes fastest.
Arguments:
- calib: bfloat16 [16, 8, 64, 8192], P('tile', None, None, 'band'), may hold values from -0.09375 to 0.09375
- support: int32 [16, 8], P('tile'), may hold values from 0 to 15, as said below
- band_window: int32 [16, 8, 2], P('tile'), may hold values from 0 to 128, as said below
- measured: float32 [1024], P('tile'), may hold values from -60 to 60
Outputs:
- solution: float32 [16, 8192], P('tile', 'band')
- residual: float32 [1024], P('tile')
The draws below stay inside these ranges and needn't reach their ends.
Inputs may be any that keep to these rules, and one draw needn't show every extreme that they name: `support`: entries 0 to 3 of each tile name blocks within 4 of the tile's own number along the cyclic order; the other entries name blocks whose index of tile (block // 2) lies 3 to 8 - 3 steps ahead of the tile's own, cyclically, and the tiles of one index of tile name at most 3 such blocks of any one other index. `band_window`: each window holds at least a quarter of the 128 bands; the first band is at most half of 128.
All inputs are finite; a program needn't handle non-finite values.
Results may differ from the reference program's by a relative error of at most 0.012.
The reference program's roundings to bfloat16 on the way count: a program that leaves them out, or rounds other values in their place, can miss the bound.
Values may be sent and summed in bfloat16 or wider, within the bound.
A program may use at most 64 MiB of HBM per device.

```python
import jax
import jax.numpy as jnp
from jax import lax

PIX = 64
BANDS = 128
K = 8
TILE_DEV = 2
ITERS = 2
TILES = 16
BLOCKS = 16
SENSOR = 1024


def draw_support(key, part):
    key_near, key_pick, key_perm = jax.random.split(key, 3)
    devices = TILES // TILE_DEV
    half = K // 2
    far_count = K - half
    spread = devices - 5
    anchor = jnp.arange(TILES, dtype=jnp.int32)[:, None]
    offset = jax.random.randint(key_near, (TILES, half), -2 * TILE_DEV, 2 * TILE_DEV + 1)
    offset = offset.at[0, 0].set(-1)
    offset = offset.at[1, 0].set(-1)
    near = (anchor + offset) % BLOCKS
    orders = jax.vmap(lambda sub: jax.random.permutation(sub, spread))(jax.random.split(key_perm, devices)).astype(jnp.int32)
    device = anchor // TILE_DEV
    position = anchor % TILE_DEV * far_count + jnp.arange(far_count, dtype=jnp.int32)[None, :]
    ahead = 3 + orders[device, position % spread]
    owner = (device + ahead) % devices
    far = owner * TILE_DEV + jax.random.randint(key_pick, (TILES, far_count), 0, TILE_DEV)
    return jnp.concatenate([near, far], axis=1).astype(jnp.int32)


def draw_band_window(key, part):
    key_start, key_len = jax.random.split(key)
    start = jax.random.randint(key_start, (TILES, K), 0, BANDS // 2)
    length = jax.random.randint(key_len, (TILES, K), BANDS // 4, BANDS // 2 + 1)
    window = jnp.stack([start, start + length], axis=2).astype(jnp.int32)
    window = window.at[0, 0, 0].set(BANDS // 2)
    window = window.at[0, 0, 1].set(BANDS)
    window = window.at[1, 0, 0].set(0)
    return window


def draw_measured(key, part):
    key_base, key_rough = jax.random.split(key)
    place = jnp.arange(SENSOR, dtype=jnp.float32) / SENSOR
    rough = jnp.exp(jnp.log(3.0) * jax.random.uniform(key_rough, (SENSOR // PIX, 1), dtype=jnp.float32))
    rough = jnp.broadcast_to(rough, (SENSOR // PIX, PIX)).reshape(SENSOR)
    base = jnp.clip(jax.random.normal(key_base, (SENSOR,), dtype=jnp.float32), -6.0, 6.0)
    rise = jnp.exp(jnp.log(3.0) * place)
    return (base * rise * rough).astype(jnp.float32)


def block_levels(own_key, shape, shards, smallest, high):
    loudness = 1.0
    for axis_at, shards_of in shards:
        draws = jax.random.uniform(jax.random.fold_in(jax.random.fold_in(own_key, 6), axis_at), (shards_of,), jnp.float32, smallest / len(shards), high / len(shards))
        loudness = loudness * jnp.repeat(jnp.exp(draws), shape[axis_at] // shards_of).reshape((-1,) + (1,) * (len(shape) - 1 - axis_at))
    return loudness


def scatter_about(stream_key, dims, scale, limit, cuts=(), held_as=jnp.bfloat16):
    drawn = jax.random.normal(stream_key, dims, jnp.float32) * scale
    if len(cuts) > 0:
        drawn = block_levels(stream_key, dims, cuts, -0.22, 0.18) * drawn
    return jnp.clip(drawn, min=-limit, max=limit).astype(held_as)


def setup_inputs(seed: int = 0) -> dict:
    seeds = jax.random.split(jax.random.key(seed), 5)
    return {
        "calib": scatter_about(seeds[0], (TILES, K, PIX, BANDS * PIX), (PIX * BANDS // 2) ** -0.5, 0.09375, ((0, 8), (3, 4))),
        "support": draw_support(jax.random.fold_in(seeds[4], 71), 0),
        "band_window": draw_band_window(jax.random.fold_in(seeds[4], 71), 0),
        "measured": draw_measured(jax.random.fold_in(seeds[4], 71), 0),
    }


ridge_weight = 0.25


def reference(calib, support, band_window, measured):
    width = BANDS * PIX
    bands = jnp.arange(width, dtype=jnp.int32) // PIX
    inside = (bands[None, None, :] >= band_window[:, :, 0:1]) & (bands[None, None, :] < band_window[:, :, 1:2])

    def forward(direction):
        blocks_b = lax.optimization_barrier(direction.astype(jnp.bfloat16)).astype(jnp.float32)

        def one_tile(args):
            rows, ids, mask = args
            picked = jnp.where(mask, blocks_b[ids], jnp.zeros((), jnp.float32))
            return jnp.einsum("kij,kj->i", rows.astype(jnp.float32), picked, precision=lax.Precision.HIGHEST)

        return lax.map(one_tile, (calib, support, inside)).reshape(-1)

    def adjoint(sensor):
        rows_b = lax.optimization_barrier(sensor.astype(jnp.bfloat16)).astype(jnp.float32).reshape(TILES, PIX)

        def one_tile(args):
            rows, vec, mask = args
            terms = jnp.einsum("kij,i->kj", rows.astype(jnp.float32), vec, precision=lax.Precision.HIGHEST)
            return jnp.where(mask, terms, jnp.zeros((), jnp.float32))

        terms = lax.map(one_tile, (calib, rows_b, inside))
        return jax.ops.segment_sum(terms.reshape(TILES * K, width), support.reshape(-1), num_segments=BLOCKS)

    residual = measured
    gradient = adjoint(measured)
    direction = gradient
    solution = jnp.zeros_like(gradient)
    gamma = jnp.sum(gradient * gradient)
    for step in range(ITERS):
        image = forward(direction)
        delta = jnp.sum(image * image) + ridge_weight * jnp.sum(direction * direction)
        alpha = gamma / delta
        solution = solution + alpha * direction
        residual = residual - alpha * image
        if step + 1 < ITERS:
            gradient = adjoint(residual) - ridge_weight * solution
            gamma_next = jnp.sum(gradient * gradient)
            direction = gradient + (gamma_next / gamma) * direction
            gamma = gamma_next
    return solution, residual
```

```python
import functools

import jax
import jax.numpy as jnp
from jax import lax
from jax.experimental import pallas as pl
from jax.experimental.pallas import tpu as pltpu
from jax.sharding import PartitionSpec as P

BANDS_PER_GROUP_PIX = 64
RIDGE = 0.25
LANES = 128
RS_TYPE = jnp.float32
MESH = pl.DeviceIdType.MESH


def kernel(
    n_tile,
    n_band,
    group,
    calib,
    support,
    window,
    measured,
    solution_out,
    residual_out,
    held,
    stage,
    rs_buf,
    ag_mine,
    ag_buf,
    sc_mine,
    sc_buf,
    blocks,
    band_buf,
    sq_mine,
    sq_buf,
    load_sem,
    tile_send,
    tile_recv,
    band_send,
    band_recv,
):
    tile_rows, k, pix, width = calib.shape
    entries = tile_rows * k
    rows = entries * pix
    n_block = n_tile * tile_rows
    me = lax.axis_index("tile")
    band = lax.axis_index("band")
    f32 = jnp.float32

    def entry_of(e):
        return e // k, e % k

    loads = []
    for e in range(entries):
        t, j = entry_of(e)
        copy = pltpu.make_async_copy(
            calib.at[t, j], held.at[pl.ds(e * pix, pix), :], load_sem.at[e]
        )
        copy.start()
        loads.append(copy)

    barrier = pltpu.get_barrier_semaphore()
    peers = [lax.rem(me + h, n_tile) for h in range(n_tile)]
    others = [lax.rem(band + h, n_band) for h in range(n_band)]
    for h in range(1, n_tile):
        pl.semaphore_signal(barrier, inc=1, device_id={"tile": peers[h]}, device_id_type=MESH)
    for h in range(1, n_band):
        pl.semaphore_signal(barrier, inc=1, device_id={"band": others[h]}, device_id_type=MESH)

    lane_entry = lax.broadcasted_iota(jnp.int32, (1, rows), 1) // pix
    sup_row = jnp.zeros((1, rows), jnp.int32)
    for e in range(entries):
        t, j = entry_of(e)
        sup_row = jnp.where(lane_entry == e, support[t, j], sup_row)
    slot = lax.broadcasted_iota(jnp.int32, (n_block, 1), 0)
    hop, part = slot // tile_rows, slot % tile_rows
    ahead = me + hop
    ahead = jnp.where(ahead >= n_tile, ahead - n_tile, ahead) * tile_rows + part
    behind = me - hop
    behind = jnp.where(behind < 0, behind + n_tile, behind) * tile_rows + part
    to_adj = jnp.broadcast_to(sup_row, (n_block, rows)) == ahead
    to_fwd = jnp.broadcast_to(sup_row, (n_block, rows)) == behind

    lane = lax.broadcasted_iota(jnp.int32, (1, LANES), 1)
    low = lane < pix

    def spread(w):
        pieces = []
        for t in range(tile_rows):
            col = t * pix // LANES * LANES
            tilev = w[:, col : col + LANES]
            rolled = pltpu.roll(tilev, pix, 1)
            both = jnp.where(low, tilev, rolled) if t * pix % LANES == 0 else jnp.where(low, rolled, tilev)
            pieces += [both] * (k * pix // LANES)
        return jnp.concatenate(pieces, axis=1)

    def left_side(w):
        wide = jnp.broadcast_to(spread(w), (n_block, rows))
        return jnp.where(to_adj, wide, jnp.zeros((), f32)).astype(jnp.bfloat16)

    def exchange_tile(phase, source, target):
        copies = []
        for h in range(1, n_tile):
            copy = pltpu.make_async_remote_copy(
                src_ref=source(h),
                dst_ref=target(h),
                send_sem=tile_send.at[phase, h],
                recv_sem=tile_recv.at[phase, h],
                device_id={"tile": peers[h]},
                device_id_type=MESH,
            )
            copy.start()
            copies.append(copy)
        return copies

    def exchange_band(phase):
        copies = []
        for h in range(1, n_band):
            copy = pltpu.make_async_remote_copy(
                src_ref=band_buf.at[phase, band],
                dst_ref=band_buf.at[phase, band],
                send_sem=band_send.at[phase, h],
                recv_sem=band_recv.at[phase, h],
                device_id={"band": others[h]},
                device_id_type=MESH,
            )
            copy.start()
            copies.append(copy)
        return copies

    def finish(copies):
        for copy in copies:
            copy.wait()

    def scatter_sum(it, phase, product):
        for h in range(n_tile):
            stage[it, h] = product[h * tile_rows : (h + 1) * tile_rows, :].astype(RS_TYPE)
        if it == 0:
            pl.semaphore_wait(barrier, n_tile + n_band - 2)
        copies = exchange_tile(phase, lambda h: stage.at[it, h], lambda h: rs_buf.at[it, h])
        total = product[0:tile_rows, :]
        for h, copy in enumerate(copies, 1):
            copy.wait()
            total = total + rs_buf[it, h].astype(f32)
        return total

    def lanes_sum(x):
        x = jnp.sum(x, axis=0, keepdims=True)
        total = x[:, 0:LANES]
        for c in range(1, width // LANES):
            total = total + x[:, c * LANES : (c + 1) * LANES]
        return total

    def gather_forward(it, phase, vector, scalars):
        packed = vector.astype(jnp.bfloat16)
        ag_mine[it] = packed
        first = exchange_tile(phase, lambda h: ag_mine.at[it], lambda h: ag_buf.at[it, h])
        for i, s in enumerate(scalars):
            sc_mine[it, i : i + 1, :] = s
        second = exchange_tile(phase + 1, lambda h: sc_mine.at[it], lambda h: sc_buf.at[it, h])
        blocks[0:tile_rows, :] = packed.astype(f32)
        for h, copy in enumerate(first, 1):
            copy.wait()
            blocks[h * tile_rows : (h + 1) * tile_rows, :] = ag_buf[it, h].astype(f32)
        out = lax.dot_general(
            blocks[...].astype(jnp.bfloat16),
            held[...],
            (((1,), (1,)), ((), ())),
            preferred_element_type=f32,
        )
        out = jnp.sum(jnp.where(to_fwd, out, jnp.zeros((), f32)), axis=0, keepdims=True)
        cols = []
        per = k * pix // LANES
        for t in range(tile_rows):
            acc = out[:, t * per * LANES : t * per * LANES + LANES]
            for c in range(1, per):
                at = (t * per + c) * LANES
                acc = acc + out[:, at : at + LANES]
            cols.append(acc + pltpu.roll(acc, pix, 1))
        image = jnp.concatenate(
            [jnp.where(low, cols[t], cols[t + 1]) for t in range(0, tile_rows, 2)], axis=1
        )
        finish(second)
        sums = sc_mine[it]
        for h in range(1, n_tile):
            sums = sums + sc_buf[it, h]
        band_buf[it, band, 0:1, :] = image
        band_buf[it, band, 1:3, :] = sums[0:2, :]
        finish(exchange_band(it))
        total = band_buf[it, 0]
        for b in range(1, n_band):
            total = total + band_buf[it, b]
        return total[0:1, :], [jnp.sum(total[i : i + 1, :], axis=1, keepdims=True) for i in (1, 2)]

    def image_square(it, phase, image):
        sq_mine[it, 0:1, :] = image * image
        copies = exchange_tile(phase, lambda h: sq_mine.at[it], lambda h: sq_buf.at[it, h])
        total = image * image
        for h, copy in enumerate(copies, 1):
            copy.wait()
            total = total + sq_buf[it, h, 0:1, :]
        return jnp.sum(total, axis=1, keepdims=True)

    for it in range(2):
        sc_mine[it] = jnp.zeros_like(sc_mine[it])
        sq_mine[it] = jnp.zeros_like(sq_mine[it])
        band_buf[it, band] = jnp.zeros_like(band_buf[it, band])

    start = measured[...]
    left = left_side(start)
    bands = band * (width // BANDS_PER_GROUP_PIX) + (
        lax.broadcasted_iota(jnp.int32, (1, width), 1) // BANDS_PER_GROUP_PIX
    )
    product = jnp.zeros((n_block, width), f32)
    for g in range(entries // group):
        for e in range(g * group, (g + 1) * group):
            t, j = entry_of(e)
            loads[e].wait()
            at = pl.ds(e * pix, pix)
            inside = jnp.where(
                (bands >= window[t, j, 0]) & (bands < window[t, j, 1]), 1.0, 0.0
            ).astype(jnp.bfloat16)
            held[at, :] = held[at, :] * inside
        span = group * pix
        product = product + jnp.dot(
            left[:, g * span : (g + 1) * span],
            held[g * span : (g + 1) * span, :],
            preferred_element_type=f32,
        )
    direction = scatter_sum(0, 0, product)

    norm = lanes_sum(direction * direction)
    image, (gamma, _) = gather_forward(0, 1, direction, [norm])
    alpha = gamma / (image_square(0, 3, image) + RIDGE * gamma)
    solved = alpha * direction
    residual = start - alpha * image

    product = jnp.dot(left_side(residual), held[...], preferred_element_type=f32)
    gradient = scatter_sum(1, 4, product) - RIDGE * solved
    partial, (gamma_next, cross) = gather_forward(
        1, 5, gradient, [lanes_sum(gradient * gradient), lanes_sum(gradient * direction)]
    )
    beta = gamma_next / gamma
    image = partial + beta * image
    square = gamma_next + 2.0 * beta * cross + beta * beta * gamma
    alpha = gamma_next / (image_square(1, 7, image) + RIDGE * square)
    solution_out[...] = solved + alpha * (gradient + beta * direction)
    residual_out[...] = residual - alpha * image


def body(calib, support, band_window, measured):
    n_tile, n_band = lax.axis_size("tile"), lax.axis_size("band")
    tile_rows, k, pix, width = calib.shape
    entries = tile_rows * k
    sensor = tile_rows * pix
    f32, bf16 = jnp.float32, jnp.bfloat16
    vmem, smem = pl.BlockSpec(memory_space=pltpu.VMEM), pl.BlockSpec(memory_space=pltpu.SMEM)
    dma = pltpu.SemaphoreType.DMA
    solved, residual = pl.pallas_call(
        functools.partial(kernel, n_tile, n_band, 4),
        out_shape=(
            jax.ShapeDtypeStruct((tile_rows, width), f32),
            jax.ShapeDtypeStruct((1, sensor), f32),
        ),
        in_specs=[pl.BlockSpec(memory_space=pl.ANY), smem, smem, vmem],
        out_specs=(vmem, vmem),
        scratch_shapes=[
            pltpu.VMEM((entries * pix, width), bf16),
            pltpu.VMEM((2, n_tile, tile_rows, width), RS_TYPE),
            pltpu.VMEM((2, n_tile, tile_rows, width), RS_TYPE),
            pltpu.VMEM((2, tile_rows, width), bf16),
            pltpu.VMEM((2, n_tile, tile_rows, width), bf16),
            pltpu.VMEM((2, 8, LANES), f32),
            pltpu.VMEM((2, n_tile, 8, LANES), f32),
            pltpu.VMEM((n_tile * tile_rows, width), f32),
            pltpu.VMEM((2, n_band, 8, sensor), f32),
            pltpu.VMEM((2, 8, sensor), f32),
            pltpu.VMEM((2, n_tile, 8, sensor), f32),
            dma((entries,)),
            dma((8, n_tile)),
            dma((8, n_tile)),
            dma((2, n_band)),
            dma((2, n_band)),
        ],
        compiler_params=pltpu.CompilerParams(collective_id=0, has_side_effects=True),
    )(calib, support, band_window, measured.reshape(1, sensor))
    return solved, residual.reshape(sensor)


def solution(mesh):
    placed = (P("tile", None, None, "band"), P("tile", None), P("tile", None, None), P("tile"))
    return jax.shard_map(
        body, mesh=mesh, in_specs=placed, out_specs=(P("tile", "band"), P("tile")), check_vma=False
    )
```

```python
import functools

import jax
import jax.numpy as jnp
from jax import lax
from jax.experimental import pallas as pl
from jax.experimental.pallas import tpu as pltpu
from jax.sharding import PartitionSpec as P

BANDS_PER_GROUP_PIX = 64
RIDGE = 0.25
LANES = 128
RS_TYPES = (jnp.float32, jnp.bfloat16)
CHUNKS = 4
MESH = pl.DeviceIdType.MESH


def kernel(
    n_tile,
    n_band,
    calib,
    support,
    window,
    measured,
    solved_out,
    step_out,
    residual_out,
    change_out,
    held,
    stage_a,
    stage_b,
    rs_a,
    rs_b,
    product_own,
    grad_buf,
    ag_mine,
    ag_buf,
    sc_mine,
    sc_buf,
    band_buf,
    sq_mine,
    sq_buf,
    load_sem,
    chunk_send,
    chunk_recv,
    tile_send,
    tile_recv,
    band_send,
    band_recv,
):
    tile_rows, k, pix, width = calib.shape
    entries = tile_rows * k
    rows = entries * pix
    n_block = n_tile * tile_rows
    me = lax.axis_index("tile")
    band = lax.axis_index("band")
    f32 = jnp.float32

    def entry_of(e):
        return e // k, e % k

    span = width // CHUNKS
    stage, rs_buf = (stage_a, stage_b), (rs_a, rs_b)

    loads = []
    for c in range(CHUNKS):
        cols = pl.ds(c * span, span)
        copies = []
        for e in range(entries):
            t, j = entry_of(e)
            copy = pltpu.make_async_copy(
                calib.at[t, j, :, cols], held.at[c, pl.ds(e * pix, pix), :], load_sem.at[c, e]
            )
            copy.start()
            copies.append(copy)
        loads.append(copies)

    barrier = pltpu.get_barrier_semaphore()
    peers = [lax.rem(me + h, n_tile) for h in range(n_tile)]
    others = [lax.rem(band + h, n_band) for h in range(n_band)]
    for h in range(1, n_tile):
        pl.semaphore_signal(barrier, inc=1, device_id={"tile": peers[h]}, device_id_type=MESH)
    for h in range(1, n_band):
        pl.semaphore_signal(barrier, inc=1, device_id={"band": others[h]}, device_id_type=MESH)

    lane_entry = lax.broadcasted_iota(jnp.int32, (1, rows), 1) // pix
    sup_row = jnp.zeros((1, rows), jnp.int32)
    for e in range(entries):
        t, j = entry_of(e)
        sup_row = jnp.where(lane_entry == e, support[t, j], sup_row)
    slot = lax.broadcasted_iota(jnp.int32, (n_block, 1), 0)
    hop, part = slot // tile_rows, slot % tile_rows
    ahead = me + hop
    ahead = jnp.where(ahead >= n_tile, ahead - n_tile, ahead) * tile_rows + part
    behind = me - hop
    behind = jnp.where(behind < 0, behind + n_tile, behind) * tile_rows + part
    to_adj = jnp.broadcast_to(sup_row, (n_block, rows)) == ahead
    to_fwd = jnp.broadcast_to(sup_row, (n_block, rows)) == behind

    lane = lax.broadcasted_iota(jnp.int32, (1, LANES), 1)
    low = lane < pix

    def spread(w):
        pieces = []
        for t in range(tile_rows):
            col = t * pix // LANES * LANES
            tilev = w[:, col : col + LANES]
            rolled = pltpu.roll(tilev, pix, 1)
            both = jnp.where(low, tilev, rolled) if t * pix % LANES == 0 else jnp.where(low, rolled, tilev)
            pieces += [both] * (k * pix // LANES)
        return jnp.concatenate(pieces, axis=1)

    def left_side(w):
        wide = jnp.broadcast_to(spread(w), (n_block, rows))
        return jnp.where(to_adj, wide, jnp.zeros((), f32)).astype(jnp.bfloat16)

    def exchange_tile(phase, source, target, sends=tile_send, recvs=tile_recv):
        copies = []
        for h in range(1, n_tile):
            copy = pltpu.make_async_remote_copy(
                src_ref=source(h),
                dst_ref=target(h),
                send_sem=sends.at[phase, h],
                recv_sem=recvs.at[phase, h],
                device_id={"tile": peers[h]},
                device_id_type=MESH,
            )
            copy.start()
            copies.append(copy)
        return copies

    def exchange_band(phase):
        copies = []
        for h in range(1, n_band):
            copy = pltpu.make_async_remote_copy(
                src_ref=band_buf.at[phase, band],
                dst_ref=band_buf.at[phase, band],
                send_sem=band_send.at[phase, h],
                recv_sem=band_recv.at[phase, h],
                device_id={"band": others[h]},
                device_id_type=MESH,
            )
            copy.start()
            copies.append(copy)
        return copies

    def finish(copies):
        for copy in copies:
            copy.wait()

    def scatter_send(it, c, product):
        for h in range(n_tile):
            stage[it][c, h] = product[h * tile_rows : (h + 1) * tile_rows, :].astype(RS_TYPES[it])
        product_own[it, c] = product[0:tile_rows, :]
        return exchange_tile(
            (2 * it) * CHUNKS + c,
            lambda h: stage[it].at[c, h],
            lambda h: rs_buf[it].at[c, h],
            chunk_send,
            chunk_recv,
        )

    def scatter_sum(it, c, copies):
        total = product_own[it, c]
        for h, copy in enumerate(copies, 1):
            copy.wait()
            total = total + rs_buf[it][c, h].astype(f32)
        return total

    def gather_send(it, c, vector):
        ag_mine[it, c] = vector.astype(jnp.bfloat16)
        return exchange_tile(
            (2 * it + 1) * CHUNKS + c,
            lambda h: ag_mine.at[it, c],
            lambda h: ag_buf.at[it, c, h],
            chunk_send,
            chunk_recv,
        )

    def lanes_sum(x):
        x = jnp.sum(x, axis=0, keepdims=True)
        total = x[:, 0:LANES]
        for c in range(1, span // LANES):
            total = total + x[:, c * LANES : (c + 1) * LANES]
        return total

    def forward(it, phase, gathers, scalars):
        for i, s in enumerate(scalars):
            sc_mine[it, i : i + 1, :] = s
        second = exchange_tile(phase, lambda h: sc_mine.at[it], lambda h: sc_buf.at[it, h])
        out = jnp.zeros((n_block, rows), f32)
        for c in range(CHUNKS):
            parts = [ag_mine[it, c].astype(f32)]
            for h, copy in enumerate(gathers[c], 1):
                copy.wait()
                parts.append(ag_buf[it, c, h].astype(f32))
            out = out + lax.dot_general(
                jnp.concatenate(parts, axis=0).astype(jnp.bfloat16),
                held[c],
                (((1,), (1,)), ((), ())),
                preferred_element_type=f32,
            )
        out = jnp.sum(jnp.where(to_fwd, out, jnp.zeros((), f32)), axis=0, keepdims=True)
        cols = []
        per = k * pix // LANES
        for t in range(tile_rows):
            acc = out[:, t * per * LANES : t * per * LANES + LANES]
            for c in range(1, per):
                at = (t * per + c) * LANES
                acc = acc + out[:, at : at + LANES]
            cols.append(acc + pltpu.roll(acc, pix, 1))
        image = jnp.concatenate(
            [jnp.where(low, cols[t], cols[t + 1]) for t in range(0, tile_rows, 2)], axis=1
        )
        finish(second)
        sums = sc_mine[it]
        for h in range(1, n_tile):
            sums = sums + sc_buf[it, h]
        band_buf[it, band, 0:1, :] = image
        band_buf[it, band, 1:3, :] = sums[0:2, :]
        finish(exchange_band(it))
        total = band_buf[it, 0]
        for b in range(1, n_band):
            total = total + band_buf[it, b]
        return total[0:1, :], [jnp.sum(total[i : i + 1, :], axis=1, keepdims=True) for i in (1, 2)]

    def image_square(it, phase, image):
        sq_mine[it, 0:1, :] = image * image
        copies = exchange_tile(phase, lambda h: sq_mine.at[it], lambda h: sq_buf.at[it, h])
        total = image * image
        for h, copy in enumerate(copies, 1):
            copy.wait()
            total = total + sq_buf[it, h, 0:1, :]
        return jnp.sum(total, axis=1, keepdims=True)

    for it in range(2):
        sc_mine[it] = jnp.zeros_like(sc_mine[it])
        sq_mine[it] = jnp.zeros_like(sq_mine[it])
        band_buf[it, band] = jnp.zeros_like(band_buf[it, band])

    start = measured[...]
    left = left_side(start)
    sends = []
    for c in range(CHUNKS):
        bands = band * (width // BANDS_PER_GROUP_PIX) + (
            (c * span + lax.broadcasted_iota(jnp.int32, (1, span), 1)) // BANDS_PER_GROUP_PIX
        )
        for e in range(entries):
            t, j = entry_of(e)
            loads[c][e].wait()
            at = pl.ds(e * pix, pix)
            inside = jnp.where(
                (bands >= window[t, 0, j]) & (bands < window[t, 1, j]), 1.0, 0.0
            ).astype(jnp.bfloat16)
            held[c, at, :] = held[c, at, :] * inside
        product = jnp.dot(left, held[c], preferred_element_type=f32)
        if c == 0:
            pl.semaphore_wait(barrier, n_tile + n_band - 2)
        sends.append(scatter_send(0, c, product))
    gathers = []
    norm = jnp.zeros((1, LANES), f32)
    for c in range(CHUNKS):
        direction = scatter_sum(0, c, sends[c])
        gathers.append(gather_send(0, c, direction))
        grad_buf[0, c] = direction
        norm = norm + lanes_sum(direction * direction)
    image, (gamma, _) = forward(0, 0, gathers, [norm])
    alpha = gamma / (image_square(0, 1, image) + RIDGE * gamma)
    residual = start - alpha * image

    left = left_side(residual)
    sends = [
        scatter_send(1, c, jnp.dot(left, held[c], preferred_element_type=f32))
        for c in range(CHUNKS)
    ]
    gathers = []
    norm, cross = jnp.zeros((1, LANES), f32), jnp.zeros((1, LANES), f32)
    for c in range(CHUNKS):
        direction = grad_buf[0, c]
        gradient = scatter_sum(1, c, sends[c]) - RIDGE * (alpha * direction)
        gathers.append(gather_send(1, c, gradient))
        grad_buf[1, c] = gradient
        norm = norm + lanes_sum(gradient * gradient)
        cross = cross + lanes_sum(gradient * direction)
    partial, (gamma_next, cross) = forward(1, 2, gathers, [norm, cross])
    beta = gamma_next / gamma
    image = partial + beta * image
    square = gamma_next + 2.0 * beta * cross + beta * beta * gamma
    step = gamma_next / (image_square(1, 3, image) + RIDGE * square)
    for c in range(CHUNKS):
        cols = pl.ds(c * span, span)
        solved_out[:, cols] = alpha * grad_buf[0, c]
        step_out[:, cols] = step * (grad_buf[1, c] + beta * grad_buf[0, c])
    residual_out[...] = residual
    change_out[...] = step * image


def finish_kernel(solved, step, residual, change, solution_out, residual_out):
    solution_out[...] = solved[...] + step[...]
    residual_out[...] = residual[...] - change[...]


def body(calib, support, band_window, measured):
    n_tile, n_band = lax.axis_size("tile"), lax.axis_size("band")
    tile_rows, k, pix, width = calib.shape
    entries = tile_rows * k
    sensor = tile_rows * pix
    f32, bf16 = jnp.float32, jnp.bfloat16
    vmem, smem = pl.BlockSpec(memory_space=pltpu.VMEM), pl.BlockSpec(memory_space=pltpu.SMEM)
    dma = pltpu.SemaphoreType.DMA
    span = width // CHUNKS
    cube = jax.ShapeDtypeStruct((tile_rows, width), f32)
    image = jax.ShapeDtypeStruct((1, sensor), f32)
    held_back = pl.pallas_call(
        functools.partial(kernel, n_tile, n_band),
        out_shape=(cube, cube, image, image),
        in_specs=[pl.BlockSpec(memory_space=pl.ANY), smem, smem, vmem],
        out_specs=(vmem,) * 4,
        scratch_shapes=[
            pltpu.VMEM((CHUNKS, entries * pix, span), bf16),
            pltpu.VMEM((CHUNKS, n_tile, tile_rows, span), RS_TYPES[0]),
            pltpu.VMEM((CHUNKS, n_tile, tile_rows, span), RS_TYPES[1]),
            pltpu.VMEM((CHUNKS, n_tile, tile_rows, span), RS_TYPES[0]),
            pltpu.VMEM((CHUNKS, n_tile, tile_rows, span), RS_TYPES[1]),
            pltpu.VMEM((2, CHUNKS, tile_rows, span), f32),
            pltpu.VMEM((2, CHUNKS, tile_rows, span), f32),
            pltpu.VMEM((2, CHUNKS, tile_rows, span), bf16),
            pltpu.VMEM((2, CHUNKS, n_tile, tile_rows, span), bf16),
            pltpu.VMEM((2, 8, LANES), f32),
            pltpu.VMEM((2, n_tile, 8, LANES), f32),
            pltpu.VMEM((2, n_band, 8, sensor), f32),
            pltpu.VMEM((2, 8, sensor), f32),
            pltpu.VMEM((2, n_tile, 8, sensor), f32),
            dma((CHUNKS, entries)),
            dma((4 * CHUNKS, n_tile)),
            dma((4 * CHUNKS, n_tile)),
            dma((4, n_tile)),
            dma((4, n_tile)),
            dma((2, n_band)),
            dma((2, n_band)),
        ],
        compiler_params=pltpu.CompilerParams(collective_id=0, has_side_effects=True),
    )(calib, support, jnp.transpose(band_window, (0, 2, 1)), measured.reshape(1, sensor))
    solved, residual = pl.pallas_call(
        finish_kernel,
        out_shape=(cube, image),
        in_specs=[vmem] * 4,
        out_specs=(vmem, vmem),
    )(*held_back)
    return solved, residual.reshape(sensor)


def solution(mesh):
    placed = (P("tile", None, None, "band"), P("tile", None), P("tile", None, None), P("tile"))
    return jax.shard_map(
        body, mesh=mesh, in_specs=placed, out_specs=(P("tile", "band"), P("tile")), check_vma=False
    )
```

```python
import functools

import jax
import jax.numpy as jnp
from jax import lax
from jax.experimental import pallas as pl
from jax.experimental.pallas import tpu as pltpu
from jax.sharding import PartitionSpec as P

BANDS_PER_GROUP_PIX = 64
RIDGE = 0.25
LANES = 128
RS_TYPES = (jnp.float32, jnp.bfloat16)
CHUNKS = 4
MESH = pl.DeviceIdType.MESH


def kernel(
    n_tile,
    n_band,
    calib,
    support,
    window,
    measured,
    solved_out,
    step_out,
    residual_out,
    change_out,
    held,
    stage_a,
    stage_b,
    rs_a,
    rs_b,
    product_own,
    grad_buf,
    ag_mine,
    ag_buf,
    all_buf,
    load_sem,
    chunk_send,
    chunk_recv,
    all_send,
    all_recv,
):
    tile_rows, k, pix, width = calib.shape
    entries = tile_rows * k
    rows = entries * pix
    n_block = n_tile * tile_rows
    me = lax.axis_index("tile")
    band = lax.axis_index("band")
    f32 = jnp.float32

    def entry_of(e):
        return e // k, e % k

    span = width // CHUNKS
    stage, rs_buf = (stage_a, stage_b), (rs_a, rs_b)

    loads = []
    for c in range(CHUNKS):
        cols = pl.ds(c * span, span)
        copies = []
        for e in range(entries):
            t, j = entry_of(e)
            copy = pltpu.make_async_copy(
                calib.at[t, j, :, cols], held.at[c, pl.ds(e * pix, pix), :], load_sem.at[c, e]
            )
            copy.start()
            copies.append(copy)
        loads.append(copies)

    barrier = pltpu.get_barrier_semaphore()
    peers = [lax.rem(me + h, n_tile) for h in range(n_tile)]
    others = [lax.rem(band + h, n_band) for h in range(n_band)]
    everyone = [(a, b) for a in range(n_tile) for b in range(n_band) if a or b]
    for a, b in everyone:
        pl.semaphore_signal(
            barrier,
            inc=1,
            device_id={"tile": peers[a], "band": others[b]},
            device_id_type=MESH,
        )

    lane_entry = lax.broadcasted_iota(jnp.int32, (1, rows), 1) // pix
    sup_row = jnp.zeros((1, rows), jnp.int32)
    for e in range(entries):
        t, j = entry_of(e)
        sup_row = jnp.where(lane_entry == e, support[t, j], sup_row)
    slot = lax.broadcasted_iota(jnp.int32, (n_block, 1), 0)
    hop, part = slot // tile_rows, slot % tile_rows
    ahead = me + hop
    ahead = jnp.where(ahead >= n_tile, ahead - n_tile, ahead) * tile_rows + part
    behind = me - hop
    behind = jnp.where(behind < 0, behind + n_tile, behind) * tile_rows + part
    to_adj = jnp.broadcast_to(sup_row, (n_block, rows)) == ahead
    to_fwd = jnp.broadcast_to(sup_row, (n_block, rows)) == behind

    lane = lax.broadcasted_iota(jnp.int32, (1, LANES), 1)
    low = lane < pix
    first_half = lane < LANES // 2

    def spread(w):
        pieces = []
        for t in range(tile_rows):
            col = t * pix // LANES * LANES
            tilev = w[:, col : col + LANES]
            rolled = pltpu.roll(tilev, pix, 1)
            both = jnp.where(low, tilev, rolled) if t * pix % LANES == 0 else jnp.where(low, rolled, tilev)
            pieces += [both] * (k * pix // LANES)
        return jnp.concatenate(pieces, axis=1)

    def left_side(w):
        wide = jnp.broadcast_to(spread(w), (n_block, rows))
        return jnp.where(to_adj, wide, jnp.zeros((), f32)).astype(jnp.bfloat16)

    def exchange_tile(phase, source, target, sends, recvs):
        copies = []
        for h in range(1, n_tile):
            copy = pltpu.make_async_remote_copy(
                src_ref=source(h),
                dst_ref=target(h),
                send_sem=sends.at[phase, h],
                recv_sem=recvs.at[phase, h],
                device_id={"tile": peers[h]},
                device_id_type=MESH,
            )
            copy.start()
            copies.append(copy)
        return copies

    def exchange_all(it):
        copies = []
        for a, b in everyone:
            copy = pltpu.make_async_remote_copy(
                src_ref=all_buf.at[it, me, band],
                dst_ref=all_buf.at[it, me, band],
                send_sem=all_send.at[it, a, b],
                recv_sem=all_recv.at[it, a, b],
                device_id={"tile": peers[a], "band": others[b]},
                device_id_type=MESH,
            )
            copy.start()
            copies.append(copy)
        return copies

    def finish(copies):
        for copy in copies:
            copy.wait()

    def scatter_send(it, c, product):
        for h in range(n_tile):
            stage[it][c, h] = product[h * tile_rows : (h + 1) * tile_rows, :].astype(RS_TYPES[it])
        product_own[it, c] = product[0:tile_rows, :]
        return exchange_tile(
            (2 * it) * CHUNKS + c,
            lambda h: stage[it].at[c, h],
            lambda h: rs_buf[it].at[c, h],
            chunk_send,
            chunk_recv,
        )

    def scatter_sum(it, c, copies):
        total = product_own[it, c]
        for h, copy in enumerate(copies, 1):
            copy.wait()
            total = total + rs_buf[it][c, h].astype(f32)
        return total

    def gather_send(it, c, vector):
        ag_mine[it, c] = vector.astype(jnp.bfloat16)
        return exchange_tile(
            (2 * it + 1) * CHUNKS + c,
            lambda h: ag_mine.at[it, c],
            lambda h: ag_buf.at[it, c, h],
            chunk_send,
            chunk_recv,
        )

    def lanes_sum(x):
        x = jnp.sum(x, axis=0, keepdims=True)
        total = x[:, 0:LANES]
        for c in range(1, span // LANES):
            total = total + x[:, c * LANES : (c + 1) * LANES]
        return total

    def forward(it, gathers, scalars):
        out = jnp.zeros((n_block, rows), f32)
        for c in range(CHUNKS):
            parts = [ag_mine[it, c].astype(f32)]
            for h, copy in enumerate(gathers[c], 1):
                copy.wait()
                parts.append(ag_buf[it, c, h].astype(f32))
            out = out + lax.dot_general(
                jnp.concatenate(parts, axis=0).astype(jnp.bfloat16),
                held[c],
                (((1,), (1,)), ((), ())),
                preferred_element_type=f32,
            )
        out = jnp.sum(jnp.where(to_fwd, out, jnp.zeros((), f32)), axis=0, keepdims=True)
        cols = []
        per = k * pix // LANES
        for t in range(tile_rows):
            acc = out[:, t * per * LANES : t * per * LANES + LANES]
            for c in range(1, per):
                at = (t * per + c) * LANES
                acc = acc + out[:, at : at + LANES]
            cols.append(acc + pltpu.roll(acc, pix, 1))
        image = jnp.concatenate(
            [jnp.where(low, cols[t], cols[t + 1]) for t in range(0, tile_rows, 2)], axis=1
        )
        halves = [x + pltpu.roll(x, LANES // 2, 1) for x in scalars]
        all_buf[it, me, band, 0:1, :] = image
        all_buf[it, me, band, 1:2, :] = jnp.where(first_half, halves[0], halves[1])
        finish(exchange_all(it))
        total = all_buf[it, :, 0]
        mine = all_buf[it, me, 0]
        for b in range(1, n_band):
            total = total + all_buf[it, :, b]
            mine = mine + all_buf[it, me, b]
        sums = jnp.sum(total, axis=0)[1:2, :]
        zero = jnp.zeros_like(sums)
        return (
            total,
            mine[0:1, :],
            jnp.sum(jnp.where(first_half, sums, zero), axis=1, keepdims=True),
            jnp.sum(jnp.where(first_half, zero, sums), axis=1, keepdims=True),
        )

    def image_square(total):
        square = jnp.sum(total * total, axis=0)[0:1, :]
        return jnp.sum(square, axis=1, keepdims=True)

    start = measured[...]
    left = left_side(start)
    products = []
    for c in range(CHUNKS):
        bands = band * (width // BANDS_PER_GROUP_PIX) + (
            (c * span + lax.broadcasted_iota(jnp.int32, (1, span), 1)) // BANDS_PER_GROUP_PIX
        )
        for e in range(entries):
            t, j = entry_of(e)
            loads[c][e].wait()
            at = pl.ds(e * pix, pix)
            inside = jnp.where(
                (bands >= window[t, 0, j]) & (bands < window[t, 1, j]), 1.0, 0.0
            ).astype(jnp.bfloat16)
            held[c, at, :] = held[c, at, :] * inside
        product = jnp.dot(left, held[c], preferred_element_type=f32)
        products.append(product)
    pl.semaphore_wait(barrier, n_tile * n_band - 1)
    sends = [scatter_send(0, c, products[c]) for c in range(CHUNKS)]
    gathers = []
    norm = jnp.zeros((1, LANES), f32)
    for c in range(CHUNKS):
        direction = scatter_sum(0, c, sends[c])
        gathers.append(gather_send(0, c, direction))
        grad_buf[0, c] = direction
        norm = norm + lanes_sum(direction * direction)
    images, image, gamma, _ = forward(0, gathers, [norm, norm])
    alpha = gamma / (image_square(images) + RIDGE * gamma)
    residual = start - alpha * image

    left = left_side(residual)
    sends = [
        scatter_send(1, c, jnp.dot(left, held[c], preferred_element_type=f32))
        for c in range(CHUNKS)
    ]
    gathers = []
    norm, cross = jnp.zeros((1, LANES), f32), jnp.zeros((1, LANES), f32)
    for c in range(CHUNKS):
        direction = grad_buf[0, c]
        gradient = scatter_sum(1, c, sends[c]) - RIDGE * (alpha * direction)
        gathers.append(gather_send(1, c, gradient))
        grad_buf[1, c] = gradient
        norm = norm + lanes_sum(gradient * gradient)
        cross = cross + lanes_sum(gradient * direction)
    partials, partial, gamma_next, cross = forward(1, gathers, [norm, cross])
    beta = gamma_next / gamma
    image = partial + beta * image
    images = partials + beta * images
    square = gamma_next + 2.0 * beta * cross + beta * beta * gamma
    step = gamma_next / (image_square(images) + RIDGE * square)
    for c in range(CHUNKS):
        cols = pl.ds(c * span, span)
        solved_out[:, cols] = alpha * grad_buf[0, c]
        step_out[:, cols] = step * (grad_buf[1, c] + beta * grad_buf[0, c])
    residual_out[...] = residual
    change_out[...] = step * image


def finish_kernel(solved, step, residual, change, solution_out, residual_out):
    solution_out[...] = solved[...] + step[...]
    residual_out[...] = residual[...] - change[...]


def body(calib, support, band_window, measured):
    n_tile, n_band = lax.axis_size("tile"), lax.axis_size("band")
    tile_rows, k, pix, width = calib.shape
    entries = tile_rows * k
    sensor = tile_rows * pix
    f32, bf16 = jnp.float32, jnp.bfloat16
    vmem, smem = pl.BlockSpec(memory_space=pltpu.VMEM), pl.BlockSpec(memory_space=pltpu.SMEM)
    dma = pltpu.SemaphoreType.DMA
    span = width // CHUNKS
    cube = jax.ShapeDtypeStruct((tile_rows, width), f32)
    image = jax.ShapeDtypeStruct((1, sensor), f32)
    held_back = pl.pallas_call(
        functools.partial(kernel, n_tile, n_band),
        out_shape=(cube, cube, image, image),
        in_specs=[pl.BlockSpec(memory_space=pl.ANY), smem, smem, vmem],
        out_specs=(vmem,) * 4,
        scratch_shapes=[
            pltpu.VMEM((CHUNKS, entries * pix, span), bf16),
            pltpu.VMEM((CHUNKS, n_tile, tile_rows, span), RS_TYPES[0]),
            pltpu.VMEM((CHUNKS, n_tile, tile_rows, span), RS_TYPES[1]),
            pltpu.VMEM((CHUNKS, n_tile, tile_rows, span), RS_TYPES[0]),
            pltpu.VMEM((CHUNKS, n_tile, tile_rows, span), RS_TYPES[1]),
            pltpu.VMEM((2, CHUNKS, tile_rows, span), f32),
            pltpu.VMEM((2, CHUNKS, tile_rows, span), f32),
            pltpu.VMEM((2, CHUNKS, tile_rows, span), bf16),
            pltpu.VMEM((2, CHUNKS, n_tile, tile_rows, span), bf16),
            pltpu.VMEM((2, n_tile, n_band, 2, sensor), f32),
            dma((CHUNKS, entries)),
            dma((4 * CHUNKS, n_tile)),
            dma((4 * CHUNKS, n_tile)),
            dma((2, n_tile, n_band)),
            dma((2, n_tile, n_band)),
        ],
        compiler_params=pltpu.CompilerParams(collective_id=0, has_side_effects=True),
    )(calib, support, jnp.transpose(band_window, (0, 2, 1)), measured.reshape(1, sensor))
    solved, residual = pl.pallas_call(
        finish_kernel,
        out_shape=(cube, image),
        in_specs=[vmem] * 4,
        out_specs=(vmem, vmem),
    )(*held_back)
    return solved, residual.reshape(sensor)


def solution(mesh):
    placed = (P("tile", None, None, "band"), P("tile", None), P("tile", None, None), P("tile"))
    return jax.shard_map(
        body, mesh=mesh, in_specs=placed, out_specs=(P("tile", "band"), P("tile")), check_vma=False
    )
```

```python
import functools

import jax
import jax.numpy as jnp
from jax import lax
from jax.experimental import pallas as pl
from jax.experimental.pallas import tpu as pltpu
from jax.sharding import PartitionSpec as P

BANDS_PER_GROUP_PIX = 64
RIDGE = 0.25
LANES = 128
RS_TYPES = (jnp.float32, jnp.bfloat16)
CHUNKS = 2
MESH = pl.DeviceIdType.MESH


def kernel(
    n_tile,
    n_band,
    calib,
    support,
    window,
    measured,
    solved_out,
    step_out,
    residual_out,
    change_out,
    held,
    stage_a,
    stage_b,
    rs_a,
    rs_b,
    product_own,
    grad_buf,
    ag_mine,
    ag_buf,
    all_buf,
    load_sem,
    chunk_send,
    chunk_recv,
    all_send,
    all_recv,
):
    tile_rows, k, pix, width = calib.shape
    entries = tile_rows * k
    rows = entries * pix
    n_block = n_tile * tile_rows
    me = lax.axis_index("tile")
    band = lax.axis_index("band")
    f32 = jnp.float32

    def entry_of(e):
        return e // k, e % k

    span = width // CHUNKS
    stage, rs_buf = (stage_a, stage_b), (rs_a, rs_b)

    loads = []
    for c in range(CHUNKS):
        cols = pl.ds(c * span, span)
        copies = []
        for e in range(entries):
            t, j = entry_of(e)
            copy = pltpu.make_async_copy(
                calib.at[t, j, :, cols], held.at[c, pl.ds(e * pix, pix), :], load_sem.at[c, e]
            )
            copy.start()
            copies.append(copy)
        loads.append(copies)

    barrier = pltpu.get_barrier_semaphore()
    peers = [lax.rem(me + h, n_tile) for h in range(n_tile)]
    others = [lax.rem(band + h, n_band) for h in range(n_band)]
    everyone = [(a, b) for a in range(n_tile) for b in range(n_band) if a or b]
    for a, b in everyone:
        pl.semaphore_signal(
            barrier,
            inc=1,
            device_id={"tile": peers[a], "band": others[b]},
            device_id_type=MESH,
        )

    lane_entry = lax.broadcasted_iota(jnp.int32, (1, rows), 1) // pix
    sup_row = jnp.zeros((1, rows), jnp.int32)
    for e in range(entries):
        t, j = entry_of(e)
        sup_row = jnp.where(lane_entry == e, support[t, j], sup_row)
    slot = lax.broadcasted_iota(jnp.int32, (n_block, 1), 0)
    hop, part = slot // tile_rows, slot % tile_rows
    ahead = me + hop
    ahead = jnp.where(ahead >= n_tile, ahead - n_tile, ahead) * tile_rows + part
    behind = me - hop
    behind = jnp.where(behind < 0, behind + n_tile, behind) * tile_rows + part
    to_adj = jnp.broadcast_to(sup_row, (n_block, rows)) == ahead
    to_fwd = jnp.broadcast_to(sup_row, (n_block, rows)) == behind

    lane = lax.broadcasted_iota(jnp.int32, (1, LANES), 1)
    low = lane < pix
    first_half = lane < LANES // 2

    def spread(w):
        pieces = []
        for t in range(tile_rows):
            col = t * pix // LANES * LANES
            tilev = w[:, col : col + LANES]
            rolled = pltpu.roll(tilev, pix, 1)
            both = jnp.where(low, tilev, rolled) if t * pix % LANES == 0 else jnp.where(low, rolled, tilev)
            pieces += [both] * (k * pix // LANES)
        return jnp.concatenate(pieces, axis=1)

    def left_side(w):
        wide = jnp.broadcast_to(spread(w), (n_block, rows))
        return jnp.where(to_adj, wide, jnp.zeros((), f32)).astype(jnp.bfloat16)

    def exchange_tile(phase, source, target, sends, recvs):
        copies = []
        for h in range(1, n_tile):
            copy = pltpu.make_async_remote_copy(
                src_ref=source(h),
                dst_ref=target(h),
                send_sem=sends.at[phase, h],
                recv_sem=recvs.at[phase, h],
                device_id={"tile": peers[h]},
                device_id_type=MESH,
            )
            copy.start()
            copies.append(copy)
        return copies

    def exchange_all(it):
        copies = []
        for a, b in everyone:
            copy = pltpu.make_async_remote_copy(
                src_ref=all_buf.at[it, me, band],
                dst_ref=all_buf.at[it, me, band],
                send_sem=all_send.at[it, a, b],
                recv_sem=all_recv.at[it, a, b],
                device_id={"tile": peers[a], "band": others[b]},
                device_id_type=MESH,
            )
            copy.start()
            copies.append(copy)
        return copies

    def finish(copies):
        for copy in copies:
            copy.wait()

    def scatter_send(it, c, product):
        for h in range(n_tile):
            stage[it][c, h] = product[h * tile_rows : (h + 1) * tile_rows, :].astype(RS_TYPES[it])
        product_own[it, c] = product[0:tile_rows, :]
        return exchange_tile(
            (2 * it) * CHUNKS + c,
            lambda h: stage[it].at[c, h],
            lambda h: rs_buf[it].at[c, h],
            chunk_send,
            chunk_recv,
        )

    def scatter_sum(it, c, copies):
        total = product_own[it, c]
        for h, copy in enumerate(copies, 1):
            copy.wait()
            total = total + rs_buf[it][c, h].astype(f32)
        return total

    def gather_send(it, c, vector):
        ag_mine[it, c] = vector.astype(jnp.bfloat16)
        return exchange_tile(
            (2 * it + 1) * CHUNKS + c,
            lambda h: ag_mine.at[it, c],
            lambda h: ag_buf.at[it, c, h],
            chunk_send,
            chunk_recv,
        )

    def lanes_sum(x):
        x = jnp.sum(x, axis=0, keepdims=True)
        total = x[:, 0:LANES]
        for c in range(1, span // LANES):
            total = total + x[:, c * LANES : (c + 1) * LANES]
        return total

    def forward(it, gathers, scalars):
        out = jnp.zeros((n_block, rows), f32)
        for c in range(CHUNKS):
            parts = [ag_mine[it, c].astype(f32)]
            for h, copy in enumerate(gathers[c], 1):
                copy.wait()
                parts.append(ag_buf[it, c, h].astype(f32))
            out = out + lax.dot_general(
                jnp.concatenate(parts, axis=0).astype(jnp.bfloat16),
                held[c],
                (((1,), (1,)), ((), ())),
                preferred_element_type=f32,
            )
        out = jnp.sum(jnp.where(to_fwd, out, jnp.zeros((), f32)), axis=0, keepdims=True)
        cols = []
        per = k * pix // LANES
        for t in range(tile_rows):
            acc = out[:, t * per * LANES : t * per * LANES + LANES]
            for c in range(1, per):
                at = (t * per + c) * LANES
                acc = acc + out[:, at : at + LANES]
            cols.append(acc + pltpu.roll(acc, pix, 1))
        image = jnp.concatenate(
            [jnp.where(low, cols[t], cols[t + 1]) for t in range(0, tile_rows, 2)], axis=1
        )
        halves = [x + pltpu.roll(x, LANES // 2, 1) for x in scalars]
        all_buf[it, me, band, 0:1, :] = image
        all_buf[it, me, band, 1:2, :] = jnp.where(first_half, halves[0], halves[1])
        finish(exchange_all(it))
        total = all_buf[it, :, 0]
        mine = all_buf[it, me, 0]
        for b in range(1, n_band):
            total = total + all_buf[it, :, b]
            mine = mine + all_buf[it, me, b]
        sums = jnp.sum(total, axis=0)[1:2, :]
        zero = jnp.zeros_like(sums)
        return (
            total,
            mine[0:1, :],
            jnp.sum(jnp.where(first_half, sums, zero), axis=1, keepdims=True),
            jnp.sum(jnp.where(first_half, zero, sums), axis=1, keepdims=True),
        )

    def image_square(total):
        square = jnp.sum(total * total, axis=0)[0:1, :]
        return jnp.sum(square, axis=1, keepdims=True)

    start = measured[...]
    left = left_side(start)
    products = []
    for c in range(CHUNKS):
        bands = band * (width // BANDS_PER_GROUP_PIX) + (
            (c * span + lax.broadcasted_iota(jnp.int32, (1, span), 1)) // BANDS_PER_GROUP_PIX
        )
        for e in range(entries):
            t, j = entry_of(e)
            loads[c][e].wait()
            at = pl.ds(e * pix, pix)
            inside = jnp.where(
                (bands >= window[t, 0, j]) & (bands < window[t, 1, j]), 1.0, 0.0
            ).astype(jnp.bfloat16)
            held[c, at, :] = held[c, at, :] * inside
        product = jnp.dot(left, held[c], preferred_element_type=f32)
        products.append(product)
    pl.semaphore_wait(barrier, n_tile * n_band - 1)
    sends = [scatter_send(0, c, products[c]) for c in range(CHUNKS)]
    gathers = []
    norm = jnp.zeros((1, LANES), f32)
    for c in range(CHUNKS):
        direction = scatter_sum(0, c, sends[c])
        gathers.append(gather_send(0, c, direction))
        grad_buf[0, c] = direction
        norm = norm + lanes_sum(direction * direction)
    images, image, gamma, _ = forward(0, gathers, [norm, norm])
    alpha = gamma / (image_square(images) + RIDGE * gamma)
    residual = start - alpha * image

    left = left_side(residual)
    sends = [
        scatter_send(1, c, jnp.dot(left, held[c], preferred_element_type=f32))
        for c in range(CHUNKS)
    ]
    gathers = []
    norm, cross = jnp.zeros((1, LANES), f32), jnp.zeros((1, LANES), f32)
    for c in range(CHUNKS):
        direction = grad_buf[0, c]
        gradient = scatter_sum(1, c, sends[c]) - RIDGE * (alpha * direction)
        gathers.append(gather_send(1, c, gradient))
        grad_buf[1, c] = gradient
        norm = norm + lanes_sum(gradient * gradient)
        cross = cross + lanes_sum(gradient * direction)
    partials, partial, gamma_next, cross = forward(1, gathers, [norm, cross])
    beta = gamma_next / gamma
    image = partial + beta * image
    images = partials + beta * images
    square = gamma_next + 2.0 * beta * cross + beta * beta * gamma
    step = gamma_next / (image_square(images) + RIDGE * square)
    for c in range(CHUNKS):
        cols = pl.ds(c * span, span)
        solved_out[:, cols] = alpha * grad_buf[0, c]
        step_out[:, cols] = step * (grad_buf[1, c] + beta * grad_buf[0, c])
    residual_out[...] = residual
    change_out[...] = step * image


def finish_kernel(solved, step, residual, change, solution_out, residual_out):
    solution_out[...] = solved[...] + step[...]
    residual_out[...] = residual[...] - change[...]


def body(calib, support, band_window, measured):
    n_tile, n_band = lax.axis_size("tile"), lax.axis_size("band")
    tile_rows, k, pix, width = calib.shape
    entries = tile_rows * k
    sensor = tile_rows * pix
    f32, bf16 = jnp.float32, jnp.bfloat16
    vmem, smem = pl.BlockSpec(memory_space=pltpu.VMEM), pl.BlockSpec(memory_space=pltpu.SMEM)
    dma = pltpu.SemaphoreType.DMA
    span = width // CHUNKS
    cube = jax.ShapeDtypeStruct((tile_rows, width), f32)
    image = jax.ShapeDtypeStruct((1, sensor), f32)
    held_back = pl.pallas_call(
        functools.partial(kernel, n_tile, n_band),
        out_shape=(cube, cube, image, image),
        in_specs=[pl.BlockSpec(memory_space=pl.ANY), smem, smem, vmem],
        out_specs=(vmem,) * 4,
        scratch_shapes=[
            pltpu.VMEM((CHUNKS, entries * pix, span), bf16),
            pltpu.VMEM((CHUNKS, n_tile, tile_rows, span), RS_TYPES[0]),
            pltpu.VMEM((CHUNKS, n_tile, tile_rows, span), RS_TYPES[1]),
            pltpu.VMEM((CHUNKS, n_tile, tile_rows, span), RS_TYPES[0]),
            pltpu.VMEM((CHUNKS, n_tile, tile_rows, span), RS_TYPES[1]),
            pltpu.VMEM((2, CHUNKS, tile_rows, span), f32),
            pltpu.VMEM((2, CHUNKS, tile_rows, span), f32),
            pltpu.VMEM((2, CHUNKS, tile_rows, span), bf16),
            pltpu.VMEM((2, CHUNKS, n_tile, tile_rows, span), bf16),
            pltpu.VMEM((2, n_tile, n_band, 2, sensor), f32),
            dma((CHUNKS, entries)),
            dma((4 * CHUNKS, n_tile)),
            dma((4 * CHUNKS, n_tile)),
            dma((2, n_tile, n_band)),
            dma((2, n_tile, n_band)),
        ],
        compiler_params=pltpu.CompilerParams(collective_id=0, has_side_effects=True),
    )(calib, support, jnp.transpose(band_window, (0, 2, 1)), measured.reshape(1, sensor))
    solved, residual = pl.pallas_call(
        finish_kernel,
        out_shape=(cube, image),
        in_specs=[vmem] * 4,
        out_specs=(vmem, vmem),
    )(*held_back)
    return solved, residual.reshape(sensor)


def solution(mesh):
    placed = (P("tile", None, None, "band"), P("tile", None), P("tile", None, None), P("tile"))
    return jax.shard_map(
        body, mesh=mesh, in_specs=placed, out_specs=(P("tile", "band"), P("tile")), check_vma=False
    )
```
